128 devices in a mesh: grp: 4 (over z), dp: 2 (over y_hi), mp: 16 (over y_lo, x, core).
Axes of the slice: x: 4, y: 4 (y_hi: 2, y_lo: 2; y = y_hi * 2 + y_lo), z: 4, core: 2. Of those that a mesh axis runs over, the one named last changes fastest.
Arguments:
- tower_features: bfloat16 [4, 4096, 4096], P('grp', 'dp', 'mp'), may hold values from -6 to 6
- doc_weight: bfloat16 [4096, 1024], P('mp'), may hold values from -6 to 6
- query_weight: bfloat16 [4096, 1024], P('mp'), may hold values from -6 to 6
- positive_ids: int32 [4096], replicated, may hold values from 0 to 12287
Outputs:
- loss: float32 [], replicated
- doc_grad: float32 [4096, 1024], P('mp')
- query_grad: float32 [4096, 1024], P('mp')
- feature_grad: bfloat16 [4, 4096, 4096], P('grp', 'dp', 'mp')
The draws below stay inside these ranges and needn't reach their ends.
All inputs are finite; a program needn't handle non-finite values.
Results may differ from the reference program's by a relative error of at most 0.003.
The reference program's roundings to bfloat16 on the way count: a program that leaves them out, or rounds other values in their place, can miss the bound.
Values may be sent and summed in bfloat16 or wider, within the bound.
No kernel may reach another device: no remote copies, remote signals or barrier semaphores. Data moves between devices by JAX's collectives and lax.ppermute only.
A program may use at most 64 MiB of HBM per device.

```python
import jax
import jax.numpy as jnp
from jax import lax

D = 4096
E = 1024
QUERIES = 4096
PASSAGES = 12288


def shared_weights(key):
    base_key = jax.random.fold_in(key, 21)
    noise_key = jax.random.fold_in(key, 22)
    base = jax.random.normal(base_key, (D, E), jnp.float32) * D ** (-0.5)
    noise = jax.random.normal(noise_key, (D, E), jnp.float32) * D ** (-0.5)
    return (base, noise)


def draw_doc_weight(key, part):
    base, noise = shared_weights(key)
    return jnp.clip(base, -6.0, 6.0).astype(jnp.bfloat16)


def draw_query_weight(key, part):
    base, noise = shared_weights(key)
    return jnp.clip(base + 0.1 * noise, -6.0, 6.0).astype(jnp.bfloat16)


def draw_tower_features(key, part):
    base = jax.random.normal(jax.random.fold_in(key, 31), (4 * QUERIES, D), jnp.float32)
    aligned = max(QUERIES // 16, 1)
    query_pick = jax.random.permutation(jax.random.fold_in(key, 32), QUERIES)[:aligned]
    pair_pick = jax.random.permutation(jax.random.fold_in(key, 33), PASSAGES // 2)[:aligned]
    first_rows = 2 * pair_pick
    twin_rows = first_rows + 1
    source = base[first_rows]
    twin_noise = jax.random.normal(jax.random.fold_in(key, 34), (aligned, D), jnp.float32)
    query_noise = jax.random.normal(jax.random.fold_in(key, 35), (aligned, D), jnp.float32)
    base = base.at[twin_rows].set(source + 0.15 * twin_noise)
    base = base.at[3 * QUERIES + query_pick].set(source + 0.1 * query_noise)
    return jnp.clip(base, -6.0, 6.0).reshape(4, QUERIES, D).astype(jnp.bfloat16)


def plant(array, rng, least, top_value):
    longest = array.shape.index(max(array.shape))
    spots = []
    for shift in (0, 1):
        where = [jax.random.randint(jax.random.fold_in(rng, axis), (), 0, length) for axis, length in enumerate(array.shape)]
        where[longest] = (where[longest] + shift) % array.shape[longest]
        spots.append(tuple(where))
    return array.at[spots[0]].set(least).at[spots[1]].set(top_value)


def setup_inputs(seed: int = 0) -> dict:
    key_of = jax.random.split(jax.random.key(seed), 5)
    return {
        "tower_features": draw_tower_features(jax.random.fold_in(key_of[4], 71), 0),
        "doc_weight": draw_doc_weight(jax.random.fold_in(key_of[4], 71), 0),
        "query_weight": draw_query_weight(jax.random.fold_in(key_of[4], 71), 0),
        "positive_ids": plant(jax.random.randint(key_of[3], (QUERIES,), 0, PASSAGES), jax.random.fold_in(key_of[3], 1), 0, PASSAGES - 1).astype(jnp.int32),
    }


inverse_temp = 200.0
epsilon_norm = 1e-06

def normalize(projected):
    row_norms = jnp.sqrt(lax.optimization_barrier(jnp.sum(projected * projected, axis=-1, keepdims=True)) + epsilon_norm)
    return (projected / row_norms, row_norms)

def back_norm(unit_rows, row_norms, grad_rows):
    inner = lax.optimization_barrier(jnp.sum(unit_rows * grad_rows, axis=-1, keepdims=True))
    return ((grad_rows - unit_rows * inner) / row_norms).astype(jnp.bfloat16)

def reference(tower_features, doc_weight, query_weight, positive_ids):
    total_q = tower_features.shape[1]
    passages = tower_features[:3].reshape(3 * total_q, D)
    queries = tower_features[3]
    passage_unit, passage_norm = normalize(jnp.dot(passages, doc_weight, preferred_element_type=jnp.float32))
    query_unit, query_norm = normalize(jnp.dot(queries, query_weight, preferred_element_type=jnp.float32))
    passage_emb = passage_unit.astype(jnp.bfloat16)
    query_emb = query_unit.astype(jnp.bfloat16)
    logits = inverse_temp * jnp.dot(query_emb, passage_emb.T, preferred_element_type=jnp.float32)
    row_top = lax.optimization_barrier(jnp.max(logits, axis=1))
    lse = row_top + jnp.log(lax.optimization_barrier(jnp.sum(jnp.exp(logits - row_top[:, None]), axis=1)))
    positive = jnp.take_along_axis(logits, positive_ids[:, None].astype(jnp.int32), axis=1)[:, 0]
    loss = jnp.mean(lse - positive)
    columns = lax.broadcasted_iota(jnp.int32, (1, 3 * total_q), 1)
    onehot = (columns == positive_ids[:, None].astype(jnp.int32)).astype(jnp.float32)
    dlogit = ((jnp.exp(logits - lse[:, None]) - onehot) / total_q).astype(jnp.bfloat16)
    dquery = inverse_temp * jnp.dot(dlogit, passage_emb, preferred_element_type=jnp.float32)
    dpassage = inverse_temp * jnp.dot(dlogit.T, query_emb, preferred_element_type=jnp.float32)
    passage_dy = back_norm(passage_unit, passage_norm, dpassage)
    query_dy = back_norm(query_unit, query_norm, dquery)
    doc_grad = jnp.dot(passages.T, passage_dy, preferred_element_type=jnp.float32)
    query_grad = jnp.dot(queries.T, query_dy, preferred_element_type=jnp.float32)
    passage_back = jnp.dot(passage_dy, doc_weight.T, preferred_element_type=jnp.float32).astype(jnp.bfloat16)
    query_back = jnp.dot(query_dy, query_weight.T, preferred_element_type=jnp.float32).astype(jnp.bfloat16)
    feature_grad = jnp.concatenate([passage_back.reshape(3, total_q, D), query_back[None]], axis=0)
    return (loss, doc_grad, query_grad, feature_grad)
```

```python
import jax
import jax.numpy as jnp
from jax import lax
from jax.sharding import Mesh
from jax.sharding import PartitionSpec as P


MP = ("yl", "x", "c")
Y = ("dp", "yl")
ZY = ("grp", "dp", "yl")

inverse_temp = 200.0
epsilon_norm = 1e-06


def fetch(array, axis, step):
    size = lax.axis_size(axis)
    return lax.ppermute(array, axis, [(k, (k - step) % size) for k in range(size)])


def one_way(array, axis, source, target):
    return lax.ppermute(array, axis, [(source, target)])


def turned(array, shift):
    n = array.shape[0]
    return lax.dynamic_slice_in_dim(jnp.concatenate([array, array]), shift, n, 0)


def part(array, index, count):
    size = array.shape[0] // count
    return lax.dynamic_slice_in_dim(array, index * size, size, 0)


def local(tower_features, doc_weight, query_weight, positive_ids):
    z = lax.axis_index("grp")
    yh, yl, x, c = (lax.axis_index(a) for a in ("dp", "yl", "x", "c"))
    y = 2 * yh + yl
    is_query = z == 3
    live = jnp.logical_not(is_query)
    features = tower_features[0]
    weight = jnp.where(is_query, query_weight, doc_weight)
    rows, feats = features.shape
    emb = weight.shape[1]
    per = rows // 16
    total_q = positive_ids.shape[0]

    weights = [weight] + [fetch(weight, "x", k) for k in (1, 2, 3)]
    mine = lax.all_to_all(features.reshape(4, rows // 4, feats), "x", 0, 0, tiled=True)
    partial = sum(
        jnp.dot(
            lax.dynamic_index_in_dim(mine, (x + k) % 4, 0, keepdims=False),
            weights[k],
            preferred_element_type=jnp.float32,
        )
        for k in range(4)
    )
    half = part(partial, c, 2) + fetch(part(partial, 1 - c, 2), "c", 1)
    summed = part(half, yl, 2) + fetch(part(half, 1 - yl, 2), "yl", 1)
    row_norms = jnp.sqrt(jnp.sum(summed * summed, axis=-1, keepdims=True) + epsilon_norm)
    unit_rows = summed / row_norms
    embedded = unit_rows.astype(jnp.bfloat16)

    passages = jnp.stack([embedded] + [fetch(embedded, "x", k) for k in (1, 2, 3)])
    passages = jnp.stack([passages, fetch(passages, "c", 1)], axis=1).reshape(8 * per, emb)
    sent = [one_way(embedded, "grp", 3, k) for k in range(3)]
    query = jnp.where(
        is_query, embedded, jnp.where(z == 0, sent[0], jnp.where(z == 1, sent[1], sent[2]))
    )
    queries = jnp.stack([query] + [fetch(query, Y, k) for k in (1, 2, 3)]).reshape(4 * per, emb)

    logits = inverse_temp * lax.dot_general(
        queries, passages, (((1,), (1,)), ((), ())), preferred_element_type=jnp.float32
    )
    ids = positive_ids.reshape(2, 4, 2, 2, per)
    ids = lax.dynamic_slice(ids, (0, x, c, 0, 0), (2, 1, 1, 2, per)).reshape(4, per)
    ids = turned(ids, y).reshape(4 * per)
    k = lax.broadcasted_iota(jnp.int32, (8, per), 0)
    i = lax.broadcasted_iota(jnp.int32, (8, per), 1)
    owner = ((x + k // 2) % 4 * 2 + (c + k) % 2) * 2 + yl
    column_ids = (z * total_q + yh * rows + owner * per + i).reshape(1, 8 * per)
    hit = ids[:, None] == column_ids
    positive_part = jnp.sum(jnp.where(hit, logits, 0.0), axis=1)
    local_top = jnp.where(live, jnp.max(logits, axis=1), -1e30)
    local_total = jnp.where(live, jnp.sum(jnp.exp(logits - local_top[:, None]), axis=1), 0.0)
    stats = jnp.stack([local_top, local_total, positive_part])
    stats = turned(stats.reshape(3, 4, per).transpose(1, 0, 2), (4 - y) % 4)
    stats = lax.all_to_all(
        jnp.broadcast_to(stats.reshape(1, 12, per), (16, 12, per)), ZY, 0, 0, tiled=True
    ).reshape(16, 4, 3, per)
    top = jnp.max(stats[:, :, 0], axis=0)
    total = jnp.sum(stats[:, :, 1] * jnp.exp(stats[:, :, 0] - top), axis=0)
    lse = top + jnp.log(total)
    loss = jnp.sum(lse - jnp.sum(stats[:, :, 2], axis=0))
    loss = jnp.broadcast_to(loss, (8, 128))
    loss = loss + fetch(loss, "c", 1)
    loss = (loss + fetch(loss, "x", 2)) + (fetch(loss, "x", 1) + fetch(loss, "x", 3))
    loss = loss[0, 0] / total_q
    lse_rows = turned(lse, y).reshape(4 * per)

    probs = jnp.where(live, jnp.exp(logits - lse_rows[:, None]), 0.0)
    dlogit = ((probs - hit.astype(jnp.float32)) / total_q).astype(jnp.bfloat16)
    dquery = jnp.dot(dlogit, passages, preferred_element_type=jnp.float32).reshape(4, per, emb)
    dquery = dquery[0] + sum(fetch(dquery[k], Y, 4 - k) for k in (1, 2, 3))
    dpassage = lax.dot_general(
        dlogit, queries, (((0,), (0,)), ((), ())), preferred_element_type=jnp.float32
    ).reshape(4, 2, per, emb)
    dpassage = dpassage[:, 0] + fetch(dpassage[:, 1], "c", 1)
    dpassage = dpassage[0] + sum(fetch(dpassage[k], "x", 4 - k) for k in (1, 2, 3))
    relay = jnp.concatenate(
        [one_way(dquery[: per // 2], "grp", 1, 0), one_way(dquery[per // 2 :], "grp", 1, 2)]
    )
    dquery = dquery + relay
    dquery = one_way(dquery, "grp", 0, 3) + one_way(dquery, "grp", 2, 3)

    grad_emb = inverse_temp * jnp.where(is_query, dquery, dpassage)
    inner = jnp.sum(unit_rows * grad_emb, axis=-1, keepdims=True)
    grad_proj = ((grad_emb - unit_rows * inner) / row_norms).astype(jnp.bfloat16)

    across = fetch(grad_proj, "yl", 1)
    pair = jnp.where(
        yl == 0,
        jnp.concatenate([grad_proj, across]),
        jnp.concatenate([across, grad_proj]),
    )
    column = jnp.stack([pair] + [fetch(pair, "x", k) for k in (1, 2, 3)])
    gathered = jnp.stack([column, fetch(column, "c", 1)], axis=1)
    gathered = gathered.reshape(rows, emb)
    placed = turned(features.reshape(4, 2, rows // 8, feats), x)
    placed = jnp.where(c == 0, placed, placed[:, ::-1]).reshape(rows, feats)
    weight_part = lax.dot_general(
        placed, gathered, (((0,), (0,)), ((), ())), preferred_element_type=jnp.float32
    )
    back = lax.dot_general(
        gathered, weight, (((1,), (1,)), ((), ())), preferred_element_type=jnp.float32
    ).astype(jnp.bfloat16)
    back = back.reshape(4, 2, rows // 8, feats)
    back = turned(jnp.where(c == 0, back, back[:, ::-1]), (4 - x) % 4)
    feature_part = back.reshape(1, rows, feats)

    share = lax.all_to_all(
        weight_part.reshape(8, feats // 8, emb), ("grp", "dp"), 0, 0, tiled=True
    )
    both = jnp.stack([jnp.sum(share[:6], axis=0), share[6] + share[7]]).astype(jnp.bfloat16)
    both = lax.all_to_all(
        jnp.broadcast_to(both[None], (8, *both.shape)), ("grp", "dp"), 0, 0, tiled=True
    )
    doc_grad = both[:, 0].reshape(feats, emb).astype(jnp.float32)
    query_grad = both[:, 1].reshape(feats, emb).astype(jnp.float32)
    return (loss, doc_grad, query_grad, feature_part)


def solution(mesh):
    split = Mesh(
        mesh.devices.reshape(mesh.shape["grp"], mesh.shape["dp"], 2, 4, 2),
        ("grp", "dp", "yl", "x", "c"),
    )
    placed = (P("grp", "dp", MP), P(MP, None), P(MP, None), P())
    return jax.shard_map(
        local,
        mesh=split,
        in_specs=placed,
        out_specs=(P(), P(MP, None), P(MP, None), P("grp", "dp", MP)),
        check_vma=False,
    )
```

```python
import jax
import jax.numpy as jnp
from jax import lax
from jax.sharding import Mesh
from jax.sharding import PartitionSpec as P


MP = ("yl", "x", "c")
Y = ("dp", "yl")
ZY = ("grp", "dp", "yl")

inverse_temp = 200.0
epsilon_norm = 1e-06


def fetch(array, axis, step):
    size = lax.axis_size(axis)
    return lax.ppermute(array, axis, [(k, (k - step) % size) for k in range(size)])


def one_way(array, axis, source, target):
    return lax.ppermute(array, axis, [(source, target)])


def turned(array, shift):
    n = array.shape[0]
    return lax.dynamic_slice_in_dim(jnp.concatenate([array, array]), shift, n, 0)


def part(array, index, count):
    size = array.shape[0] // count
    return lax.dynamic_slice_in_dim(array, index * size, size, 0)


def local(tower_features, doc_weight, query_weight, positive_ids):
    z = lax.axis_index("grp")
    yh, yl, x, c = (lax.axis_index(a) for a in ("dp", "yl", "x", "c"))
    y = 2 * yh + yl
    is_query = z == 3
    live = jnp.logical_not(is_query)
    features = tower_features[0]
    weight = jnp.where(is_query, query_weight, doc_weight)
    rows, feats = features.shape
    emb = weight.shape[1]
    per = rows // 16
    total_q = positive_ids.shape[0]

    outer = lax.ppermute(weight, Y, [(k, 3 - k) for k in range(4)])
    other = fetch(weight, "c", 1)
    outer_other = fetch(outer, "c", 1)
    mine = lax.all_to_all(features.reshape(4, rows // 4, feats), ("yl", "c"), 0, 0, tiled=True)
    sources = ((2 * yl + c, weight), (2 * yl + 1 - c, other))
    sources += ((2 - 2 * yl + c, outer), (3 - 2 * yl - c, outer_other))
    partial = sum(
        jnp.dot(
            lax.dynamic_index_in_dim(mine, k, 0, keepdims=False),
            w,
            preferred_element_type=jnp.float32,
        )
        for k, w in sources
    )
    summed = part(partial, x, 4) + sum(
        fetch(part(partial, (x - k) % 4, 4), "x", k) for k in (1, 2, 3)
    )
    row_norms = jnp.sqrt(jnp.sum(summed * summed, axis=-1, keepdims=True) + epsilon_norm)
    unit_rows = summed / row_norms
    embedded = unit_rows.astype(jnp.bfloat16)

    passages = jnp.stack([embedded] + [fetch(embedded, "x", k) for k in (1, 2, 3)])
    passages = jnp.stack([passages, fetch(passages, "c", 1)], axis=1).reshape(8 * per, emb)
    sent = [one_way(embedded, "grp", 3, k) for k in range(3)]
    query = jnp.where(
        is_query, embedded, jnp.where(z == 0, sent[0], jnp.where(z == 1, sent[1], sent[2]))
    )
    queries = jnp.stack([query] + [fetch(query, Y, k) for k in (1, 2, 3)]).reshape(4 * per, emb)

    logits = inverse_temp * lax.dot_general(
        queries, passages, (((1,), (1,)), ((), ())), preferred_element_type=jnp.float32
    )
    ids = positive_ids.reshape(2, 2, 2, 4, per)
    ids = lax.dynamic_slice(ids, (0, 0, c, x, 0), (2, 2, 1, 1, per)).reshape(4, per)
    ids = turned(ids, y).reshape(4 * per)
    k = lax.broadcasted_iota(jnp.int32, (8, per), 0)
    i = lax.broadcasted_iota(jnp.int32, (8, per), 1)
    owner = (yl * 2 + (c + k) % 2) * 4 + (x + k // 2) % 4
    column_ids = (z * total_q + yh * rows + owner * per + i).reshape(1, 8 * per)
    hit = ids[:, None] == column_ids
    positive_part = jnp.sum(jnp.where(hit, logits, 0.0), axis=1)
    local_top = jnp.where(live, jnp.max(logits, axis=1), -1e30)
    local_total = jnp.where(live, jnp.sum(jnp.exp(logits - local_top[:, None]), axis=1), 0.0)
    stats = jnp.stack([local_top, local_total, positive_part])
    stats = turned(stats.reshape(3, 4, per).transpose(1, 0, 2), (4 - y) % 4)
    stats = lax.all_to_all(
        jnp.broadcast_to(stats.reshape(1, 12, per), (16, 12, per)), ZY, 0, 0, tiled=True
    ).reshape(16, 4, 3, per)
    top = jnp.max(stats[:, :, 0], axis=0)
    total = jnp.sum(stats[:, :, 1] * jnp.exp(stats[:, :, 0] - top), axis=0)
    lse = top + jnp.log(total)
    loss = jnp.sum(lse - jnp.sum(stats[:, :, 2], axis=0))
    loss = jnp.broadcast_to(loss, (8, 128))
    loss = loss + fetch(loss, "c", 1)
    loss = (loss + fetch(loss, "x", 2)) + (fetch(loss, "x", 1) + fetch(loss, "x", 3))
    loss = loss[0, 0] / total_q
    lse_rows = turned(lse, y).reshape(4 * per)

    probs = jnp.where(live, jnp.exp(logits - lse_rows[:, None]), 0.0)
    dlogit = ((probs - hit.astype(jnp.float32)) / total_q).astype(jnp.bfloat16)
    dquery = jnp.dot(dlogit, passages, preferred_element_type=jnp.float32)
    dpassage = lax.dot_general(
        dlogit, queries, (((0,), (0,)), ((), ())), preferred_element_type=jnp.float32
    )
    dquery, dpassage = lax.optimization_barrier((dquery, dpassage))
    dquery = dquery.reshape(4, per, emb)
    dpassage = dpassage.reshape(4, 2, per, emb)
    dpassage = dpassage[:, 0] + fetch(dpassage[:, 1], "c", 1)
    with jax.named_scope("dq_y"):
        dq_parts = [fetch(dquery[k], Y, 4 - k) for k in (1, 2, 3)]
    with jax.named_scope("dp_x"):
        dp_parts = [fetch(dpassage[k], "x", 4 - k) for k in (1, 2, 3)]
    dquery = dquery[0] + sum(dq_parts)
    dpassage = dpassage[0] + sum(dp_parts)
    relay = jnp.concatenate(
        [one_way(dquery[: per // 2], "grp", 1, 0), one_way(dquery[per // 2 :], "grp", 1, 2)]
    )
    dquery = dquery + relay
    dquery = one_way(dquery, "grp", 0, 3) + one_way(dquery, "grp", 2, 3)

    grad_emb = inverse_temp * jnp.where(is_query, dquery, dpassage)
    inner = jnp.sum(unit_rows * grad_emb, axis=-1, keepdims=True)
    grad_proj = ((grad_emb - unit_rows * inner) / row_norms).astype(jnp.bfloat16)

    left, right = grad_proj[:, : emb // 2], grad_proj[:, emb // 2 :]
    with jax.named_scope("left_y"):
        left = jnp.stack([left, fetch(left, "yl", 1)])
    with jax.named_scope("right_x"):
        right = jnp.stack([right] + [fetch(right, "x", k) for k in (1, 2, 3)])
    with jax.named_scope("left_x"):
        left = jnp.stack([left] + [fetch(left, "x", k) for k in (1, 2, 3)], axis=1)
    with jax.named_scope("right_y"):
        right = jnp.stack([right, fetch(right, "yl", 1)])
    left = jnp.stack([left, fetch(left, "c", 1)]).reshape(rows, emb // 2)
    right = jnp.stack([right, fetch(right, "c", 1)]).reshape(rows, emb // 2)
    placed = features.reshape(2, 2, 4, per, feats)
    placed = jnp.where(yl == 0, placed, placed[::-1]).transpose(1, 0, 2, 3, 4)
    placed = jnp.where(c == 0, placed, placed[::-1]).transpose(2, 0, 1, 3, 4)
    placed = turned(placed, x).transpose(1, 2, 0, 3, 4).reshape(rows, feats)
    weight_part = jnp.concatenate(
        [
            lax.dot_general(
                placed, g, (((0,), (0,)), ((), ())), preferred_element_type=jnp.float32
            )
            for g in (left, right)
        ],
        axis=1,
    )
    back = sum(
        lax.dot_general(g, w, (((1,), (1,)), ((), ())), preferred_element_type=jnp.float32)
        for g, w in ((left, weight[:, : emb // 2]), (right, weight[:, emb // 2 :]))
    ).astype(jnp.bfloat16)
    back = back.reshape(2, 2, 4, per, feats).transpose(2, 0, 1, 3, 4)
    back = turned(back, (4 - x) % 4).transpose(1, 2, 0, 3, 4)
    back = jnp.where(c == 0, back, back[::-1]).transpose(1, 0, 2, 3, 4)
    back = jnp.where(yl == 0, back, back[::-1])
    feature_part = back.reshape(1, rows, feats)

    share = lax.all_to_all(
        weight_part.reshape(8, feats // 8, emb), ("grp", "dp"), 0, 0, tiled=True
    )
    both = jnp.stack([jnp.sum(share[:6], axis=0), share[6] + share[7]]).astype(jnp.bfloat16)
    both = lax.all_to_all(
        jnp.broadcast_to(both[None], (8, *both.shape)), ("grp", "dp"), 0, 0, tiled=True
    )
    doc_grad = both[:, 0].reshape(feats, emb).astype(jnp.float32)
    query_grad = both[:, 1].reshape(feats, emb).astype(jnp.float32)
    return (loss, doc_grad, query_grad, feature_part)


def solution(mesh):
    split = Mesh(
        mesh.devices.reshape(mesh.shape["grp"], mesh.shape["dp"], 2, 4, 2),
        ("grp", "dp", "yl", "x", "c"),
    )
    placed = (P("grp", "dp", MP), P(MP, None), P(MP, None), P())
    return jax.shard_map(
        local,
        mesh=split,
        in_specs=placed,
        out_specs=(P(), P(MP, None), P(MP, None), P("grp", "dp", MP)),
        check_vma=False,
    )
```

```python
import jax
import jax.numpy as jnp
from jax import lax
from jax.sharding import Mesh
from jax.sharding import PartitionSpec as P


MP = ("yl", "x", "c")
Y = ("dp", "yl")
ZY = ("grp", "dp", "yl")

inverse_temp = 200.0
epsilon_norm = 1e-06
dq_unit = 2.0**26
dp_unit = 2.0**17


def fetch(array, axis, step):
    size = lax.axis_size(axis)
    return lax.ppermute(array, axis, [(k, (k - step) % size) for k in range(size)])


def one_way(array, axis, source, target):
    return lax.ppermute(array, axis, [(source, target)])


def turned(array, shift):
    n = array.shape[0]
    return lax.dynamic_slice_in_dim(jnp.concatenate([array, array]), shift, n, 0)


def part(array, index, count):
    size = array.shape[0] // count
    return lax.dynamic_slice_in_dim(array, index * size, size, 0)


def local(tower_features, doc_weight, query_weight, positive_ids):
    z = lax.axis_index("grp")
    yh, yl, x, c = (lax.axis_index(a) for a in ("dp", "yl", "x", "c"))
    y = 2 * yh + yl
    is_query = z == 3
    live = jnp.logical_not(is_query)
    features = tower_features[0]
    weight = jnp.where(is_query, query_weight, doc_weight)
    rows, feats = features.shape
    emb = weight.shape[1]
    per = rows // 16
    total_q = positive_ids.shape[0]

    outer = lax.ppermute(weight, Y, [(k, 3 - k) for k in range(4)])
    other = fetch(weight, "c", 1)
    outer_other = fetch(outer, "c", 1)
    mine = lax.all_to_all(features.reshape(4, rows // 4, feats), ("yl", "c"), 0, 0, tiled=True)
    sources = ((2 * yl + c, weight), (2 * yl + 1 - c, other))
    sources += ((2 - 2 * yl + c, outer), (3 - 2 * yl - c, outer_other))
    partial = sum(
        jnp.dot(
            lax.dynamic_index_in_dim(mine, k, 0, keepdims=False),
            w,
            preferred_element_type=jnp.float32,
        )
        for k, w in sources
    )
    summed = part(partial, x, 4) + sum(
        fetch(part(partial, (x - k) % 4, 4), "x", k) for k in (1, 2, 3)
    )
    row_norms = jnp.sqrt(jnp.sum(summed * summed, axis=-1, keepdims=True) + epsilon_norm)
    unit_rows = summed / row_norms
    embedded = unit_rows.astype(jnp.bfloat16)

    sent = [one_way(embedded, "grp", 3, k) for k in range(3)]
    passages = jnp.stack([embedded] + [fetch(embedded, "x", k) for k in (1, 2, 3)])
    swapped = fetch(passages, "c", 1)
    passages = jnp.stack([passages, swapped], axis=1).reshape(8 * per, emb)
    query = jnp.where(
        is_query, embedded, jnp.where(z == 0, sent[0], jnp.where(z == 1, sent[1], sent[2]))
    )
    around = [fetch(query, Y, k) for k in (1, 2, 3)]
    queries = jnp.stack([query] + around).reshape(4 * per, emb)

    logits = inverse_temp * lax.dot_general(
        queries, passages, (((1,), (1,)), ((), ())), preferred_element_type=jnp.float32
    )
    ids = positive_ids.reshape(2, 2, 2, 4, per)
    ids = lax.dynamic_slice(ids, (0, 0, c, x, 0), (2, 2, 1, 1, per)).reshape(4, per)
    ids = turned(ids, y).reshape(4 * per)
    k = lax.broadcasted_iota(jnp.int32, (8, per), 0)
    i = lax.broadcasted_iota(jnp.int32, (8, per), 1)
    owner = (yl * 2 + (c + k) % 2) * 4 + (x + k // 2) % 4
    column_ids = (z * total_q + yh * rows + owner * per + i).reshape(1, 8 * per)
    hit = ids[:, None] == column_ids
    positive_part = jnp.sum(jnp.where(hit, logits, 0.0), axis=1)
    local_top = jnp.where(live, jnp.max(logits, axis=1), -1e30)
    local_total = jnp.where(live, jnp.sum(jnp.exp(logits - local_top[:, None]), axis=1), 0.0)
    stats = jnp.stack([local_top, local_total, positive_part])
    stats = turned(stats.reshape(3, 4, per).transpose(1, 0, 2), (4 - y) % 4)
    stats = lax.all_to_all(
        jnp.broadcast_to(stats.reshape(1, 12, per), (16, 12, per)), ZY, 0, 0, tiled=True
    ).reshape(16, 4, 3, per)
    top = jnp.max(stats[:, :, 0], axis=0)
    total = jnp.sum(stats[:, :, 1] * jnp.exp(stats[:, :, 0] - top), axis=0)
    lse = top + jnp.log(total)
    loss = jnp.sum(lse - jnp.sum(stats[:, :, 2], axis=0))
    loss = jnp.broadcast_to(loss, (8, 128))
    loss = loss + fetch(loss, "c", 1)
    loss = (loss + fetch(loss, "x", 2)) + (fetch(loss, "x", 1) + fetch(loss, "x", 3))
    loss = loss[0, 0] / total_q
    lse_rows = turned(lse, y).reshape(4 * per)

    probs = jnp.where(live, jnp.exp(logits - lse_rows[:, None]), 0.0)
    dlogit = ((probs - hit.astype(jnp.float32)) / total_q).astype(jnp.bfloat16)
    dquery = jnp.dot(dlogit, passages, preferred_element_type=jnp.float32)
    dpassage = lax.dot_general(
        dlogit, queries, (((0,), (0,)), ((), ())), preferred_element_type=jnp.float32
    )
    dquery, dpassage = lax.optimization_barrier((dquery, dpassage))
    dquery = dquery.reshape(4, per, emb)
    dpassage = dpassage.reshape(4, 2, per, emb)
    dpassage = dpassage[:, 0] + fetch(dpassage[:, 1], "c", 1)
    dq_parts = [
        fetch((dquery[k] * dq_unit).astype(jnp.float16), Y, 4 - k).astype(jnp.float32)
        for k in (1, 2, 3)
    ]
    dp_parts = [
        fetch((dpassage[k] * dp_unit).astype(jnp.float16), "x", 4 - k).astype(jnp.float32)
        for k in (1, 2, 3)
    ]
    dquery = dquery[0] * dq_unit + sum(dq_parts)
    dpassage = dpassage[0] * dp_unit + sum(dp_parts)
    half = dquery.astype(jnp.float16)
    dquery = sum(one_way(half, "grp", k, 3).astype(jnp.float32) for k in range(3))

    grad_emb = inverse_temp * jnp.where(is_query, dquery / dq_unit, dpassage / dp_unit)
    inner = jnp.sum(unit_rows * grad_emb, axis=-1, keepdims=True)
    grad_proj = ((grad_emb - unit_rows * inner) / row_norms).astype(jnp.bfloat16)

    left, right = grad_proj[:, : emb // 2], grad_proj[:, emb // 2 :]
    left = jnp.stack([left, fetch(left, "yl", 1)])
    right = jnp.stack([right] + [fetch(right, "x", k) for k in (1, 2, 3)])
    left = jnp.stack([left] + [fetch(left, "x", k) for k in (1, 2, 3)], axis=1)
    right = jnp.stack([right, fetch(right, "yl", 1)])
    left = jnp.stack([left, fetch(left, "c", 1)]).reshape(rows, emb // 2)
    right = jnp.stack([right, fetch(right, "c", 1)]).reshape(rows, emb // 2)
    placed = features.reshape(2, 2, 4, per, feats)
    placed = jnp.where(yl == 0, placed, placed[::-1]).transpose(1, 0, 2, 3, 4)
    placed = jnp.where(c == 0, placed, placed[::-1]).transpose(2, 0, 1, 3, 4)
    placed = turned(placed, x).transpose(1, 2, 0, 3, 4).reshape(rows, feats)
    weight_part = jnp.concatenate(
        [
            lax.dot_general(
                placed, g, (((0,), (0,)), ((), ())), preferred_element_type=jnp.float32
            )
            for g in (left, right)
        ],
        axis=1,
    )
    back = sum(
        lax.dot_general(g, w, (((1,), (1,)), ((), ())), preferred_element_type=jnp.float32)
        for g, w in ((left, weight[:, : emb // 2]), (right, weight[:, emb // 2 :]))
    ).astype(jnp.bfloat16)
    back = back.reshape(2, 2, 4, per, feats).transpose(2, 0, 1, 3, 4)
    back = turned(back, (4 - x) % 4).transpose(1, 2, 0, 3, 4)
    back = jnp.where(c == 0, back, back[::-1]).transpose(1, 0, 2, 3, 4)
    back = jnp.where(yl == 0, back, back[::-1])
    feature_part = back.reshape(1, rows, feats)

    share = lax.all_to_all(
        weight_part.reshape(8, feats // 8, emb), ("grp", "dp"), 0, 0, tiled=True
    )
    both = jnp.stack([jnp.sum(share[:6], axis=0), share[6] + share[7]]).astype(jnp.bfloat16)
    both = lax.all_to_all(
        jnp.broadcast_to(both[None], (8, *both.shape)), ("grp", "dp"), 0, 0, tiled=True
    )
    doc_grad = both[:, 0].reshape(feats, emb).astype(jnp.float32)
    query_grad = both[:, 1].reshape(feats, emb).astype(jnp.float32)
    return (loss, doc_grad, query_grad, feature_part)


def solution(mesh):
    split = Mesh(
        mesh.devices.reshape(mesh.shape["grp"], mesh.shape["dp"], 2, 4, 2),
        ("grp", "dp", "yl", "x", "c"),
    )
    placed = (P("grp", "dp", MP), P(MP, None), P(MP, None), P())
    return jax.shard_map(
        local,
        mesh=split,
        in_specs=placed,
        out_specs=(P(), P(MP, None), P(MP, None), P("grp", "dp", MP)),
        check_vma=False,
    )
```

```python
import jax
import jax.numpy as jnp
from jax import lax
from jax.experimental import pallas as pl
from jax.experimental.pallas import tpu as pltpu
from jax.sharding import Mesh
from jax.sharding import PartitionSpec as P


MP = ("yl", "x", "c")
Y = ("dp", "yl")
ZY = ("grp", "dp", "yl")

inverse_temp = 200.0
epsilon_norm = 1e-06
dq_unit = 2.0**26
dp_unit = 2.0**17


def fetch(array, axis, step):
    size = lax.axis_size(axis)
    return lax.ppermute(array, axis, [(k, (k - step) % size) for k in range(size)])


def one_way(array, axis, source, target):
    return lax.ppermute(array, axis, [(source, target)])


def turned(array, shift):
    n = array.shape[0]
    return lax.dynamic_slice_in_dim(jnp.concatenate([array, array]), shift, n, 0)


def part(array, index, count):
    size = array.shape[0] // count
    return lax.dynamic_slice_in_dim(array, index * size, size, 0)


def row_order_kernel(at, *refs):
    *pieces, out = refs
    lefts, rights = pieces[:8], pieces[8:]
    per, half = lefts[0].shape[1:]

    def rows(side, core, along):
        block = ((at[0] + side) % 2 * 2 + (at[1] + core) % 2) * 4 + (at[2] + along) % 4
        return pl.ds(pl.multiple_of(block * per, per), per)

    for core in range(2):
        for side in range(2):
            for k in range(4):
                out[rows(side, core, k), :half] = lefts[core * 4 + k][side]
                out[rows(side, core, k), half:] = rights[core * 2 + side][k]


def in_row_order(at, lefts, rights):
    per, half = lefts[0].shape[1:]
    vmem = pl.BlockSpec(memory_space=pltpu.VMEM)
    return pl.pallas_call(
        row_order_kernel,
        out_shape=jax.ShapeDtypeStruct((16 * per, 2 * half), lefts[0].dtype),
        in_specs=[pl.BlockSpec(memory_space=pltpu.SMEM)] + [vmem] * 12,
        out_specs=vmem,
        cost_estimate=pl.CostEstimate(
            flops=0, bytes_accessed=64 * per * half * 2, transcendentals=0
        ),
        compiler_params=pltpu.CompilerParams(vmem_limit_bytes=12 * 2**20),
    )(at, *lefts, *rights)


def summed_copies_kernel(share, out):
    doc = ((share[0] + share[1]) + (share[2] + share[3])) + (share[4] + share[5])
    doc = doc.astype(out.dtype)
    query = (share[6] + share[7]).astype(out.dtype)
    for k in range(8):
        out[k, 0] = doc
        out[k, 1] = query


def summed_copies(share):
    vmem = pl.BlockSpec(memory_space=pltpu.VMEM)
    n, rows, emb = share.shape
    return pl.pallas_call(
        summed_copies_kernel,
        out_shape=jax.ShapeDtypeStruct((n, 2, rows, emb), jnp.bfloat16),
        in_specs=[vmem],
        out_specs=vmem,
        cost_estimate=pl.CostEstimate(
            flops=share.size, bytes_accessed=share.size * 8, transcendentals=0
        ),
        compiler_params=pltpu.CompilerParams(vmem_limit_bytes=6 * 2**20),
    )(share)


def widened_kernel(both, doc, query):
    n, _, rows, _ = both.shape
    for k in range(n):
        doc[k * rows : (k + 1) * rows, :] = both[k, 0].astype(jnp.float32)
        query[k * rows : (k + 1) * rows, :] = both[k, 1].astype(jnp.float32)


def widened(both):
    vmem = pl.BlockSpec(memory_space=pltpu.VMEM)
    n, _, rows, emb = both.shape
    return pl.pallas_call(
        widened_kernel,
        out_shape=[jax.ShapeDtypeStruct((n * rows, emb), jnp.float32)] * 2,
        in_specs=[vmem],
        out_specs=[vmem] * 2,
        cost_estimate=pl.CostEstimate(
            flops=0, bytes_accessed=both.size * 6, transcendentals=0
        ),
        compiler_params=pltpu.CompilerParams(vmem_limit_bytes=6 * 2**20),
    )(both)


def local(tower_features, doc_weight, query_weight, positive_ids):
    z = lax.axis_index("grp")
    yh, yl, x, c = (lax.axis_index(a) for a in ("dp", "yl", "x", "c"))
    y = 2 * yh + yl
    is_query = z == 3
    live = jnp.logical_not(is_query)
    features = tower_features[0]
    weight = jnp.where(is_query, query_weight, doc_weight)
    rows, feats = features.shape
    emb = weight.shape[1]
    per = rows // 16
    total_q = positive_ids.shape[0]

    outer = lax.ppermute(weight, Y, [(k, 3 - k) for k in range(4)])
    other = fetch(weight, "c", 1)
    outer_other = fetch(outer, "c", 1)
    mine = lax.all_to_all(features.reshape(4, rows // 4, feats), ("yl", "c"), 0, 0, tiled=True)
    sources = ((2 * yl + c, weight), (2 * yl + 1 - c, other))
    sources += ((2 - 2 * yl + c, outer), (3 - 2 * yl - c, outer_other))
    partial = sum(
        jnp.dot(
            lax.dynamic_index_in_dim(mine, k, 0, keepdims=False),
            w,
            preferred_element_type=jnp.float32,
        )
        for k, w in sources
    )
    summed = part(partial, x, 4) + sum(
        fetch(part(partial, (x - k) % 4, 4), "x", k) for k in (1, 2, 3)
    )
    row_norms = jnp.sqrt(jnp.sum(summed * summed, axis=-1, keepdims=True) + epsilon_norm)
    unit_rows = summed / row_norms
    embedded = unit_rows.astype(jnp.bfloat16)

    sent = [one_way(embedded, "grp", 3, k) for k in range(3)]
    passages = jnp.stack([embedded] + [fetch(embedded, "x", k) for k in (1, 2, 3)])
    swapped = fetch(passages, "c", 1)
    passages = jnp.stack([passages, swapped], axis=1).reshape(8 * per, emb)
    query = jnp.where(
        is_query, embedded, jnp.where(z == 0, sent[0], jnp.where(z == 1, sent[1], sent[2]))
    )
    around = [fetch(query, Y, k) for k in (1, 2, 3)]
    queries = jnp.stack([query] + around).reshape(4 * per, emb)

    logits = inverse_temp * lax.dot_general(
        queries, passages, (((1,), (1,)), ((), ())), preferred_element_type=jnp.float32
    )
    ids = positive_ids.reshape(2, 2, 2, 4, per)
    ids = lax.dynamic_slice(ids, (0, 0, c, x, 0), (2, 2, 1, 1, per)).reshape(4, per)
    ids = turned(ids, y).reshape(4 * per)
    k = lax.broadcasted_iota(jnp.int32, (8, per), 0)
    i = lax.broadcasted_iota(jnp.int32, (8, per), 1)
    owner = (yl * 2 + (c + k) % 2) * 4 + (x + k // 2) % 4
    column_ids = (z * total_q + yh * rows + owner * per + i).reshape(1, 8 * per)
    hit = ids[:, None] == column_ids
    positive_part = jnp.sum(jnp.where(hit, logits, 0.0), axis=1)
    local_top = jnp.where(live, jnp.max(logits, axis=1), -1e30)
    local_total = jnp.where(live, jnp.sum(jnp.exp(logits - local_top[:, None]), axis=1), 0.0)
    stats = jnp.stack([local_top, local_total, positive_part])
    stats = turned(stats.reshape(3, 4, per).transpose(1, 0, 2), (4 - y) % 4)
    stats = lax.all_to_all(
        jnp.broadcast_to(stats.reshape(1, 12, per), (16, 12, per)), ZY, 0, 0, tiled=True
    ).reshape(16, 4, 3, per)
    top = jnp.max(stats[:, :, 0], axis=0)
    total = jnp.sum(stats[:, :, 1] * jnp.exp(stats[:, :, 0] - top), axis=0)
    lse = top + jnp.log(total)
    loss = jnp.sum(lse - jnp.sum(stats[:, :, 2], axis=0))
    loss = jnp.broadcast_to(loss, (8, 128))
    loss = loss + fetch(loss, "c", 1)
    losses = [fetch(loss, "x", k) for k in (1, 2, 3)]
    loss = (loss + losses[1]) + (losses[0] + losses[2])
    loss = loss[0, 0] / total_q
    lse_rows = turned(lse, y).reshape(4 * per)

    probs = jnp.where(live, jnp.exp(logits - lse_rows[:, None]), 0.0)
    dlogit = ((probs - hit.astype(jnp.float32)) / total_q).astype(jnp.bfloat16)
    dquery = jnp.dot(dlogit, passages, preferred_element_type=jnp.float32)
    dpassage = lax.dot_general(
        dlogit, queries, (((0,), (0,)), ((), ())), preferred_element_type=jnp.float32
    )
    dquery, dpassage = lax.optimization_barrier((dquery, dpassage))
    dquery = dquery.reshape(4, per, emb)
    dpassage = dpassage.reshape(4, 2, per, emb)
    dpassage = dpassage[:, 0] + fetch(dpassage[:, 1], "c", 1)
    dq_parts = [
        fetch((dquery[k] * dq_unit).astype(jnp.float16), Y, 4 - k).astype(jnp.float32)
        for k in (1, 2, 3)
    ]
    dp_parts = [
        fetch((dpassage[k] * dp_unit).astype(jnp.float16), "x", 4 - k).astype(jnp.float32)
        for k in (1, 2, 3)
    ]
    dquery = dquery[0] * dq_unit + sum(dq_parts)
    dpassage = dpassage[0] * dp_unit + sum(dp_parts)
    half = dquery.astype(jnp.float16)
    dquery = sum(one_way(half, "grp", k, 3).astype(jnp.float32) for k in range(3))

    grad_emb = inverse_temp * jnp.where(is_query, dquery / dq_unit, dpassage / dp_unit)
    inner = jnp.sum(unit_rows * grad_emb, axis=-1, keepdims=True)
    grad_proj = ((grad_emb - unit_rows * inner) / row_norms).astype(jnp.bfloat16)

    left, right = grad_proj[:, : emb // 2], grad_proj[:, emb // 2 :]
    left = jnp.stack([left, fetch(left, "yl", 1)])
    right = jnp.stack([right] + [fetch(right, "x", k) for k in (1, 2, 3)])
    lefts = [left] + [fetch(left, "x", k) for k in (1, 2, 3)]
    rights = [right, fetch(right, "yl", 1)]
    lefts += [fetch(p, "c", 1) for p in lefts]
    rights += [fetch(p, "c", 1) for p in rights]
    gathered = in_row_order(jnp.stack([yl, c, x]), lefts, rights)
    weight_part = lax.dot_general(
        features, gathered, (((0,), (0,)), ((), ())), preferred_element_type=jnp.float32
    )
    feature_part = lax.dot_general(
        gathered, weight, (((1,), (1,)), ((), ())), preferred_element_type=jnp.float32
    ).astype(jnp.bfloat16)[None]

    share = lax.all_to_all(
        weight_part.reshape(8, feats // 8, emb), ("grp", "dp"), 0, 0, tiled=True
    )
    both = lax.all_to_all(summed_copies(share), ("grp", "dp"), 0, 0, tiled=True)
    doc_grad, query_grad = widened(both)
    return (loss, doc_grad, query_grad, feature_part)


def solution(mesh):
    split = Mesh(
        mesh.devices.reshape(mesh.shape["grp"], mesh.shape["dp"], 2, 4, 2),
        ("grp", "dp", "yl", "x", "c"),
    )
    placed = (P("grp", "dp", MP), P(MP, None), P(MP, None), P())
    return jax.shard_map(
        local,
        mesh=split,
        in_specs=placed,
        out_specs=(P(), P(MP, None), P(MP, None), P("grp", "dp", MP)),
        check_vma=False,
    )
```

```python
import jax
import jax.numpy as jnp
from jax import lax
from jax.experimental import pallas as pl
from jax.experimental.pallas import tpu as pltpu
from jax.sharding import Mesh
from jax.sharding import PartitionSpec as P


MP = ("yl", "x", "c")
Y = ("dp", "yl")
ZY = ("grp", "dp", "yl")

inverse_temp = 200.0
epsilon_norm = 1e-06
dq_unit = 2.0**26
dp_unit = 2.0**17


def fetch(array, axis, step):
    size = lax.axis_size(axis)
    return lax.ppermute(array, axis, [(k, (k - step) % size) for k in range(size)])


def one_way(array, axis, source, target):
    return lax.ppermute(array, axis, [(source, target)])


def turned(array, shift):
    n = array.shape[0]
    return lax.dynamic_slice_in_dim(jnp.concatenate([array, array]), shift, n, 0)


def row_order_kernel(at, *refs):
    *pieces, out = refs
    lefts, rights = pieces[:8], pieces[8:]
    per, half = lefts[0].shape[1:]

    def rows(side, core, along):
        block = ((at[0] + side) % 2 * 2 + (at[1] + core) % 2) * 4 + (at[2] + along) % 4
        return pl.ds(pl.multiple_of(block * per, per), per)

    for core in range(2):
        for side in range(2):
            for k in range(4):
                out[rows(side, core, k), :half] = lefts[core * 4 + k][side]
                out[rows(side, core, k), half:] = rights[core * 2 + side][k]


def in_row_order(at, lefts, rights):
    per, half = lefts[0].shape[1:]
    vmem = pl.BlockSpec(memory_space=pltpu.VMEM)
    return pl.pallas_call(
        row_order_kernel,
        out_shape=jax.ShapeDtypeStruct((16 * per, 2 * half), lefts[0].dtype),
        in_specs=[pl.BlockSpec(memory_space=pltpu.SMEM)] + [vmem] * 12,
        out_specs=vmem,
        cost_estimate=pl.CostEstimate(
            flops=0, bytes_accessed=64 * per * half * 2, transcendentals=0
        ),
        compiler_params=pltpu.CompilerParams(vmem_limit_bytes=12 * 2**20),
    )(at, *lefts, *rights)


def summed_copies_kernel(share, out):
    doc = ((share[0] + share[1]) + (share[2] + share[3])) + (share[4] + share[5])
    doc = doc.astype(out.dtype)
    query = (share[6] + share[7]).astype(out.dtype)
    for k in range(8):
        out[k, 0] = doc
        out[k, 1] = query


def summed_copies(share):
    vmem = pl.BlockSpec(memory_space=pltpu.VMEM)
    n, rows, emb = share.shape
    return pl.pallas_call(
        summed_copies_kernel,
        out_shape=jax.ShapeDtypeStruct((n, 2, rows, emb), jnp.bfloat16),
        in_specs=[vmem],
        out_specs=vmem,
        cost_estimate=pl.CostEstimate(
            flops=share.size, bytes_accessed=share.size * 8, transcendentals=0
        ),
        compiler_params=pltpu.CompilerParams(vmem_limit_bytes=6 * 2**20),
    )(share)


def widened_kernel(both, doc, query):
    n, _, rows, _ = both.shape
    for k in range(n):
        doc[k * rows : (k + 1) * rows, :] = both[k, 0].astype(jnp.float32)
        query[k * rows : (k + 1) * rows, :] = both[k, 1].astype(jnp.float32)


def widened(both):
    vmem = pl.BlockSpec(memory_space=pltpu.VMEM)
    n, _, rows, emb = both.shape
    return pl.pallas_call(
        widened_kernel,
        out_shape=[jax.ShapeDtypeStruct((n * rows, emb), jnp.float32)] * 2,
        in_specs=[vmem],
        out_specs=[vmem] * 2,
        cost_estimate=pl.CostEstimate(
            flops=0, bytes_accessed=both.size * 6, transcendentals=0
        ),
        compiler_params=pltpu.CompilerParams(vmem_limit_bytes=6 * 2**20),
    )(both)


def local(tower_features, doc_weight, query_weight, positive_ids):
    z = lax.axis_index("grp")
    yh, yl, x, c = (lax.axis_index(a) for a in ("dp", "yl", "x", "c"))
    y = 2 * yh + yl
    is_query = z == 3
    live = jnp.logical_not(is_query)
    features = tower_features[0]
    weight = jnp.where(is_query, query_weight, doc_weight)
    rows, feats = features.shape
    emb = weight.shape[1]
    per = rows // 16
    total_q = positive_ids.shape[0]

    outer = lax.ppermute(weight, Y, [(k, 3 - k) for k in range(4)])
    other = fetch(weight, "c", 1)
    outer_other = fetch(outer, "c", 1)
    mine = features.reshape(4, rows // 4, feats)
    mine = lax.all_to_all(mine, ("yl", "c"), 0, 0, tiled=True)
    sources = ((2 * yl + c, weight), (2 * yl + 1 - c, other))
    sources += ((2 - 2 * yl + c, outer), (3 - 2 * yl - c, outer_other))
    partial = sum(
        jnp.dot(
            lax.dynamic_index_in_dim(mine, k, 0, keepdims=False),
            w,
            preferred_element_type=jnp.float32,
        )
        for k, w in sources
    )
    halves = partial.reshape(4, 2, per // 2, emb)

    def piece(k, h):
        return lax.dynamic_index_in_dim(halves[:, h], (x - k) % 4, 0, keepdims=False)

    units, norms, embeds = [], [], []
    for h in (0, 1):
        arrived = [fetch(piece(k, h), "x", k) for k in (1, 2, 3)]
        summed = piece(0, h) + sum(arrived)
        row_norms = jnp.sqrt(jnp.sum(summed * summed, axis=-1, keepdims=True) + epsilon_norm)
        units.append(summed / row_norms)
        norms.append(row_norms)
        embeds.append(units[h].astype(jnp.bfloat16))

    sent = []
    for h in (0, 1):
        sent.append([one_way(embeds[h], "grp", 3, k) for k in range(3)])
    sent = [jnp.concatenate(both) for both in zip(*sent)]
    embedded = lax.optimization_barrier(jnp.concatenate(embeds))
    query = jnp.where(
        is_query, embedded, jnp.where(z == 0, sent[0], jnp.where(z == 1, sent[1], sent[2]))
    )
    around = [fetch(query, Y, k) for k in (1, 2, 3)]
    queries = jnp.stack([query] + around).reshape(4 * per, emb)
    passages = jnp.stack([embedded] + [fetch(embedded, "x", k) for k in (1, 2, 3)])
    swapped = fetch(passages, "c", 1)
    passages = jnp.stack([passages, swapped]).reshape(8 * per, emb)

    logits = inverse_temp * lax.dot_general(
        queries, passages, (((1,), (1,)), ((), ())), preferred_element_type=jnp.float32
    )
    ids = positive_ids.reshape(2, 2, 2, 4, per)
    ids = lax.dynamic_slice(ids, (0, 0, c, x, 0), (2, 2, 1, 1, per)).reshape(4, per)
    ids = turned(ids, y).reshape(4 * per)
    k = lax.broadcasted_iota(jnp.int32, (8, per), 0)
    i = lax.broadcasted_iota(jnp.int32, (8, per), 1)
    owner = (yl * 2 + (c + k // 4) % 2) * 4 + (x + k) % 4
    column_ids = (z * total_q + yh * rows + owner * per + i).reshape(1, 8 * per)
    hit = ids[:, None] == column_ids
    positive_part = jnp.sum(jnp.where(hit, logits, 0.0), axis=1)
    local_top = jnp.where(live, jnp.max(logits, axis=1), -1e30)
    local_total = jnp.where(live, jnp.sum(jnp.exp(logits - local_top[:, None]), axis=1), 0.0)
    stats = jnp.stack([local_top, local_total, positive_part])
    stats = turned(stats.reshape(3, 4, per).transpose(1, 0, 2), (4 - y) % 4)
    stats = lax.all_to_all(
        jnp.broadcast_to(stats.reshape(1, 12, per), (16, 12, per)), ZY, 0, 0, tiled=True
    ).reshape(16, 4, 3, per)
    top = jnp.max(stats[:, :, 0], axis=0)
    total = jnp.sum(stats[:, :, 1] * jnp.exp(stats[:, :, 0] - top), axis=0)
    lse = top + jnp.log(total)
    loss = jnp.sum(lse - jnp.sum(stats[:, :, 2], axis=0))
    loss = jnp.broadcast_to(loss, (8, 128))
    loss = loss + fetch(loss, "c", 1)
    losses = [fetch(loss, "x", k) for k in (1, 2, 3)]
    loss = (loss + losses[1]) + (losses[0] + losses[2])
    loss = loss[0, 0] / total_q
    lse_rows = turned(lse, y).reshape(4 * per)

    probs = jnp.where(live, jnp.exp(logits - lse_rows[:, None]), 0.0)
    dlogit = ((probs - hit.astype(jnp.float32)) / total_q).astype(jnp.bfloat16)
    dquery = jnp.dot(dlogit, passages, preferred_element_type=jnp.float32)
    dpassage = lax.dot_general(
        dlogit, queries, (((0,), (0,)), ((), ())), preferred_element_type=jnp.float32
    )
    dquery, dpassage = lax.optimization_barrier((dquery, dpassage))
    dquery = dquery.reshape(4, per, emb)
    dpassage = dpassage.reshape(2, 4, per, emb)
    dpassage = dpassage[0] + fetch(dpassage[1], "c", 1)
    dq_parts = [
        fetch((dquery[k] * dq_unit).astype(jnp.float16), Y, 4 - k).astype(jnp.float32)
        for k in (1, 2, 3)
    ]
    dp_parts = [
        fetch((dpassage[k] * dp_unit).astype(jnp.float16), "x", 4 - k).astype(jnp.float32)
        for k in (1, 2, 3)
    ]
    dquery = dquery[0] * dq_unit + sum(dq_parts)
    dpassage = dpassage[0] * dp_unit + sum(dp_parts)
    half = dquery.astype(jnp.float16)
    dquery = sum(one_way(half, "grp", k, 3).astype(jnp.float32) for k in range(3))

    grad_emb = inverse_temp * jnp.where(is_query, dquery / dq_unit, dpassage / dp_unit)
    grad_halves = []
    for unit_rows, row_norms, g in zip(units, norms, jnp.split(grad_emb, 2)):
        inner = jnp.sum(unit_rows * g, axis=-1, keepdims=True)
        grad_halves.append(((g - unit_rows * inner) / row_norms).astype(jnp.bfloat16))
    grad_proj = jnp.concatenate(grad_halves)

    left, right = grad_proj[:, : emb // 2], grad_proj[:, emb // 2 :]
    left = jnp.stack([left, fetch(left, "yl", 1)])
    right = jnp.stack([right] + [fetch(right, "x", k) for k in (1, 2, 3)])
    lefts = [left] + [fetch(left, "x", k) for k in (1, 2, 3)]
    rights = [right, fetch(right, "yl", 1)]
    lefts += [fetch(p, "c", 1) for p in lefts]
    rights += [fetch(p, "c", 1) for p in rights]
    gathered = in_row_order(jnp.stack([yl, c, x]), lefts, rights)
    weight_part = lax.dot_general(
        features, gathered, (((0,), (0,)), ((), ())), preferred_element_type=jnp.float32
    )
    feature_part = lax.dot_general(
        gathered, weight, (((1,), (1,)), ((), ())), preferred_element_type=jnp.float32
    ).astype(jnp.bfloat16)[None]

    share = lax.all_to_all(
        weight_part.reshape(8, feats // 8, emb), ("grp", "dp"), 0, 0, tiled=True
    )
    both = lax.all_to_all(summed_copies(share), ("grp", "dp"), 0, 0, tiled=True)
    doc_grad, query_grad = widened(both)
    return (loss, doc_grad, query_grad, feature_part)


def solution(mesh):
    split = Mesh(
        mesh.devices.reshape(mesh.shape["grp"], mesh.shape["dp"], 2, 4, 2),
        ("grp", "dp", "yl", "x", "c"),
    )
    placed = (P("grp", "dp", MP), P(MP, None), P(MP, None), P())
    return jax.shard_map(
        local,
        mesh=split,
        in_specs=placed,
        out_specs=(P(), P(MP, None), P(MP, None), P("grp", "dp", MP)),
        check_vma=False,
    )
```

```python
import jax
import jax.numpy as jnp
from jax import lax
from jax.experimental import pallas as pl
from jax.experimental.pallas import tpu as pltpu
from jax.sharding import Mesh
from jax.sharding import PartitionSpec as P


MP = ("yl", "x", "c")
Y = ("dp", "yl")
ZY = ("grp", "dp", "yl")

inverse_temp = 200.0
epsilon_norm = 1e-06
dq_unit = 2.0**26
dp_unit = 2.0**17


def fetch(array, axis, step):
    size = lax.axis_size(axis)
    return lax.ppermute(array, axis, [(k, (k - step) % size) for k in range(size)])


def one_way(array, axis, source, target):
    return lax.ppermute(array, axis, [(source, target)])


def turned(array, shift):
    n = array.shape[0]
    return lax.dynamic_slice_in_dim(jnp.concatenate([array, array]), shift, n, 0)


def part(array, index, count):
    size = array.shape[0] // count
    return lax.dynamic_slice_in_dim(array, index * size, size, 0)


def row_order_kernel(at, *refs):
    *pieces, out = refs
    lefts, rights = pieces[:8], pieces[8:]
    per, half = lefts[0].shape[1:]

    def rows(side, core, along):
        block = ((at[0] + side) % 2 * 2 + (at[1] + core) % 2) * 4 + (at[2] + along) % 4
        return pl.ds(pl.multiple_of(block * per, per), per)

    for core in range(2):
        for side in range(2):
            for k in range(4):
                out[rows(side, core, k), :half] = lefts[core * 4 + k][side]
                out[rows(side, core, k), half:] = rights[core * 2 + side][k]


def in_row_order(at, lefts, rights):
    per, half = lefts[0].shape[1:]
    vmem = pl.BlockSpec(memory_space=pltpu.VMEM)
    return pl.pallas_call(
        row_order_kernel,
        out_shape=jax.ShapeDtypeStruct((16 * per, 2 * half), lefts[0].dtype),
        in_specs=[pl.BlockSpec(memory_space=pltpu.SMEM)] + [vmem] * 12,
        out_specs=vmem,
        cost_estimate=pl.CostEstimate(
            flops=0, bytes_accessed=64 * per * half * 2, transcendentals=0
        ),
        compiler_params=pltpu.CompilerParams(vmem_limit_bytes=12 * 2**20),
    )(at, *lefts, *rights)


def summed_copies_kernel(share, out):
    doc = ((share[0] + share[1]) + (share[2] + share[3])) + (share[4] + share[5])
    doc = doc.astype(out.dtype)
    query = (share[6] + share[7]).astype(out.dtype)
    for k in range(8):
        out[k, 0] = doc
        out[k, 1] = query


def summed_copies(share):
    vmem = pl.BlockSpec(memory_space=pltpu.VMEM)
    n, rows, emb = share.shape
    return pl.pallas_call(
        summed_copies_kernel,
        out_shape=jax.ShapeDtypeStruct((n, 2, rows, emb), jnp.bfloat16),
        in_specs=[vmem],
        out_specs=vmem,
        cost_estimate=pl.CostEstimate(
            flops=share.size, bytes_accessed=share.size * 8, transcendentals=0
        ),
        compiler_params=pltpu.CompilerParams(vmem_limit_bytes=6 * 2**20),
    )(share)


def widened_kernel(both, doc, query):
    n, _, rows, _ = both.shape
    for k in range(n):
        doc[k * rows : (k + 1) * rows, :] = both[k, 0].astype(jnp.float32)
        query[k * rows : (k + 1) * rows, :] = both[k, 1].astype(jnp.float32)


def widened(both):
    vmem = pl.BlockSpec(memory_space=pltpu.VMEM)
    n, _, rows, emb = both.shape
    return pl.pallas_call(
        widened_kernel,
        out_shape=[jax.ShapeDtypeStruct((n * rows, emb), jnp.float32)] * 2,
        in_specs=[vmem],
        out_specs=[vmem] * 2,
        cost_estimate=pl.CostEstimate(
            flops=0, bytes_accessed=both.size * 6, transcendentals=0
        ),
        compiler_params=pltpu.CompilerParams(vmem_limit_bytes=6 * 2**20),
    )(both)


def local(tower_features, doc_weight, query_weight, positive_ids):
    z = lax.axis_index("grp")
    yh, yl, x, c = (lax.axis_index(a) for a in ("dp", "yl", "x", "c"))
    y = 2 * yh + yl
    is_query = z == 3
    live = jnp.logical_not(is_query)
    features = tower_features[0]
    weight = jnp.where(is_query, query_weight, doc_weight)
    rows, feats = features.shape
    emb = weight.shape[1]
    per = rows // 16
    total_q = positive_ids.shape[0]

    outer = lax.ppermute(weight, Y, [(k, 3 - k) for k in range(4)])
    other = fetch(weight, "c", 1)
    outer_other = fetch(outer, "c", 1)
    mine = [part(features, 2 * yl + c, 4)]
    mine.append(fetch(part(features, 2 * yl + 1 - c, 4), "c", 1))
    mine.append(fetch(part(features, 2 - 2 * yl + c, 4), "yl", 1))
    mine.append(
        lax.ppermute(part(features, 3 - 2 * yl - c, 4), ("yl", "c"), [(k, 3 - k) for k in range(4)])
    )
    partial = sum(
        jnp.dot(f, w, preferred_element_type=jnp.float32)
        for f, w in zip(mine, (weight, other, outer, outer_other))
    )
    halves = partial.reshape(4, 2, per // 2, emb)

    def piece(k, h):
        return lax.dynamic_index_in_dim(halves[:, h], (x - k) % 4, 0, keepdims=False)

    units, norms, embeds = [], [], []
    for h in (0, 1):
        arrived = [fetch(piece(k, h), "x", k) for k in (1, 2, 3)]
        summed = piece(0, h) + sum(arrived)
        row_norms = jnp.sqrt(jnp.sum(summed * summed, axis=-1, keepdims=True) + epsilon_norm)
        units.append(summed / row_norms)
        norms.append(row_norms)
        embeds.append(units[h].astype(jnp.bfloat16))

    sent = []
    for h in (0, 1):
        sent.append([one_way(embeds[h], "grp", 3, k) for k in range(3)])
    sent = [jnp.concatenate(both) for both in zip(*sent)]
    embedded = lax.optimization_barrier(jnp.concatenate(embeds))
    query = jnp.where(
        is_query, embedded, jnp.where(z == 0, sent[0], jnp.where(z == 1, sent[1], sent[2]))
    )
    around = [fetch(query, Y, k) for k in (1, 2, 3)]
    queries = jnp.stack([query] + around).reshape(4 * per, emb)
    passages = jnp.stack([embedded] + [fetch(embedded, "x", k) for k in (1, 2, 3)])
    swapped = fetch(passages, "c", 1)
    passages = jnp.stack([passages, swapped]).reshape(8 * per, emb)

    logits = inverse_temp * lax.dot_general(
        queries, passages, (((1,), (1,)), ((), ())), preferred_element_type=jnp.float32
    )
    ids = positive_ids.reshape(2, 2, 2, 4, per)
    ids = lax.dynamic_slice(ids, (0, 0, c, x, 0), (2, 2, 1, 1, per)).reshape(4, per)
    ids = turned(ids, y).reshape(4 * per)
    k = lax.broadcasted_iota(jnp.int32, (8, per), 0)
    i = lax.broadcasted_iota(jnp.int32, (8, per), 1)
    owner = (yl * 2 + (c + k // 4) % 2) * 4 + (x + k) % 4
    column_ids = (z * total_q + yh * rows + owner * per + i).reshape(1, 8 * per)
    hit = ids[:, None] == column_ids
    positive_part = jnp.sum(jnp.where(hit, logits, 0.0), axis=1)
    local_top = jnp.where(live, jnp.max(logits, axis=1), -1e30)
    local_total = jnp.where(live, jnp.sum(jnp.exp(logits - local_top[:, None]), axis=1), 0.0)
    stats = jnp.stack([local_top, local_total, positive_part])
    stats = turned(stats.reshape(3, 4, per).transpose(1, 0, 2), (4 - y) % 4)
    stats = lax.all_to_all(
        jnp.broadcast_to(stats.reshape(1, 12, per), (16, 12, per)), ZY, 0, 0, tiled=True
    ).reshape(16, 4, 3, per)
    top = jnp.max(stats[:, :, 0], axis=0)
    total = jnp.sum(stats[:, :, 1] * jnp.exp(stats[:, :, 0] - top), axis=0)
    lse = top + jnp.log(total)
    loss = jnp.sum(lse - jnp.sum(stats[:, :, 2], axis=0))
    loss = jnp.broadcast_to(loss, (8, 128))
    loss = loss + fetch(loss, "c", 1)
    losses = [fetch(loss, "x", k) for k in (1, 2, 3)]
    loss = (loss + losses[1]) + (losses[0] + losses[2])
    loss = loss[0, 0] / total_q
    lse_rows = turned(lse, y).reshape(4 * per)

    probs = jnp.where(live, jnp.exp(logits - lse_rows[:, None]), 0.0)
    dlogit = ((probs - hit.astype(jnp.float32)) / total_q).astype(jnp.bfloat16)
    dlogit = lax.optimization_barrier(dlogit)
    dquery = jnp.dot(dlogit, passages, preferred_element_type=jnp.float32)
    dpassage = lax.dot_general(
        dlogit, queries, (((0,), (0,)), ((), ())), preferred_element_type=jnp.float32
    )
    dquery, dpassage = lax.optimization_barrier((dquery, dpassage))
    dquery = dquery.reshape(4, per, emb)
    dpassage = dpassage.reshape(2, 4, per, emb)
    dpassage = dpassage[0] + fetch(dpassage[1], "c", 1)
    dq_parts = [
        fetch((dquery[k] * dq_unit).astype(jnp.float16), Y, 4 - k).astype(jnp.float32)
        for k in (1, 2, 3)
    ]
    dp_parts = [
        fetch((dpassage[k] * dp_unit).astype(jnp.float16), "x", 4 - k).astype(jnp.float32)
        for k in (1, 2, 3)
    ]
    dquery = dquery[0] * dq_unit + sum(dq_parts)
    dpassage = dpassage[0] * dp_unit + sum(dp_parts)
    half = dquery.astype(jnp.float16)
    dquery = sum(one_way(half, "grp", k, 3).astype(jnp.float32) for k in range(3))

    grad_emb = inverse_temp * jnp.where(is_query, dquery / dq_unit, dpassage / dp_unit)
    grad_halves = []
    for unit_rows, row_norms, g in zip(units, norms, jnp.split(grad_emb, 2)):
        inner = jnp.sum(unit_rows * g, axis=-1, keepdims=True)
        grad_halves.append(((g - unit_rows * inner) / row_norms).astype(jnp.bfloat16))
    grad_proj = jnp.concatenate(grad_halves)

    left, right = grad_proj[:, : emb // 2], grad_proj[:, emb // 2 :]
    left = jnp.stack([left, fetch(left, "yl", 1)])
    right = jnp.stack([right] + [fetch(right, "x", k) for k in (1, 2, 3)])
    lefts = [left] + [fetch(left, "x", k) for k in (1, 2, 3)]
    rights = [right, fetch(right, "yl", 1)]
    lefts += [fetch(p, "c", 1) for p in lefts]
    rights += [fetch(p, "c", 1) for p in rights]
    gathered = in_row_order(jnp.stack([yl, c, x]), lefts, rights)
    weight_part = lax.dot_general(
        features, gathered, (((0,), (0,)), ((), ())), preferred_element_type=jnp.float32
    )
    feature_part = lax.dot_general(
        gathered, weight, (((1,), (1,)), ((), ())), preferred_element_type=jnp.float32
    ).astype(jnp.bfloat16)[None]

    share = lax.all_to_all(
        weight_part.reshape(8, feats // 8, emb), ("grp", "dp"), 0, 0, tiled=True
    )
    both = lax.all_to_all(summed_copies(share), ("grp", "dp"), 0, 0, tiled=True)
    doc_grad, query_grad = widened(both)
    return (loss, doc_grad, query_grad, feature_part)


def solution(mesh):
    split = Mesh(
        mesh.devices.reshape(mesh.shape["grp"], mesh.shape["dp"], 2, 4, 2),
        ("grp", "dp", "yl", "x", "c"),
    )
    placed = (P("grp", "dp", MP), P(MP, None), P(MP, None), P())
    return jax.shard_map(
        local,
        mesh=split,
        in_specs=placed,
        out_specs=(P(), P(MP, None), P(MP, None), P("grp", "dp", MP)),
        check_vma=False,
    )
```
